32 devices in a mesh: tile: 8 (over z, y), depth: 4 (over x, core).
Axes of the slice: x: 2, y: 2, z: 4, core: 2. Of those that a mesh axis runs over, the one named last changes fastest.
Arguments:
- positions: float32 [3, 16384], P(None, 'tile'), may hold values from -4 to 4
- log_scales: float32 [3, 16384], P(None, 'tile'), may hold values from -2 to 0
- opacity_logits: float32 [1, 16384], P(None, 'tile'), may hold values from -3 to 1.5
- colors: float32 [3, 16384], P(None, 'tile'), may hold values from 0 to 1
- first_moment: float32 [10, 16384], P(None, 'tile'), may hold values from -3 to 3
- second_moment: float32 [10, 16384], P(None, 'tile'), may hold values from 0.01 to 1
- cameras: float32 [4, 2, 4], replicated, may hold values from -6.4 to 6.4
- background: float32 [3], replicated, may hold values from 0 to 1
- target: float32 [32, 3, 1024], P('tile'), may hold values from 0 to 1
- tile_view: int32 [32], P('tile'), may hold values from 0 to 3
- tile_length: int32 [32], P('tile'), may hold values from 128 to 512
- list_owner: int32 [4, 32, 128, 1], P('depth', 'tile'), may hold values from 0 to 7; in each aligned block of 512 rows (0 to 511, 512 to 1023, ..., all dimensions but the last counted through in order) at most 160 rows name the same one
- list_row: int32 [4, 32, 128], P('depth', 'tile'), may hold values from 0 to 2047
Outputs:
- image: float32 [32, 3, 1024], P('tile')
- new_params: float32 [10, 16384], P(None, 'tile')
- new_first: float32 [10, 16384], P(None, 'tile')
- new_second: float32 [10, 16384], P(None, 'tile')
The draws below stay inside these ranges and needn't reach their ends.
Inputs may be any that keep to these rules, and one draw needn't show every extreme that they name: `list_owner`: within the entries of one device's block (one depth slab of the tiles of one tile index), no owner is named more than 160 times, a bound that some block reaches.
All inputs are finite; a program needn't handle non-finite values.
Results may differ from the reference program's by a relative error of at most 0.00008.
Values sent between devices are 32-bit elements; how exact they have to be, the bound alone decides.
A program may use at most 64 MiB of HBM per device.

```python
import math
import jax
import jax.numpy as jnp
import numpy as np
from jax import lax

TILE_SIDE = 32
PIX = 1024
LIST = 512
VIEWS = 4
TILES_DEV = 4
G_DEV = 2048
TILES = 32
SPLATS = 16384
SLAB = 128
CAP = 160
N_TILE = 8
N_DEPTH = 4


def with_ends(drawn, rng, smallest, top_value):
    spot = [jax.random.randint(jax.random.fold_in(rng, axis), (), 0, length) for axis, length in enumerate(drawn.shape)]
    main_axis = drawn.shape.index(max(drawn.shape))
    neighbour = spot[:main_axis] + [(spot[main_axis] + 1) % drawn.shape[main_axis]] + spot[main_axis + 1:]
    return drawn.at[tuple(spot)].set(smallest).at[tuple(neighbour)].set(top_value)


def shard_levels(rng, extent, shards, least, top_value):
    level = 1.0
    for dim, blocks in shards:
        draws = jax.random.uniform(jax.random.fold_in(jax.random.fold_in(rng, 6), dim), (blocks,), jnp.float32, least / len(shards), top_value / len(shards))
        level = level * jnp.repeat(jnp.exp(draws), extent[dim] // blocks).reshape((-1,) + (1,) * (len(extent) - 1 - dim))
    return level


def deal_out(key, own, number, rows, count, top, limit, slope):
    order = jax.random.permutation(key, count)
    crowded, usual = portions_of(count, rows * top, limit, slope, True), portions_of(count, rows * top, limit, slope, False)
    places = jnp.arange(count)

    def named(tallies, turn):
        used = int((tallies > 0).sum())
        fixed = max(1, used // 4)
        passed = fixed + (places - fixed + turn * (used - fixed)) % max(1, count - fixed)
        return jnp.zeros((count,), jnp.int32).at[order[jnp.where(places < fixed, places, passed)]].set(jnp.asarray(tallies, jnp.int32))

    tallies = jnp.where(number % 4 == 0, named(crowded, number // 4), named(usual, number - number // 4 - 1))
    mixed = jax.random.permutation(jax.random.fold_in(own, 3), count)
    donor, sink = mixed[0:count // 2 * 2:2], mixed[1:count // 2 * 2:2]
    margin = jnp.minimum(tallies[donor] - 1, limit - tallies[sink]) // 2
    margin = jnp.where((donor == order[0]) | (sink == order[0]) | (tallies[sink] == 0), 0, jnp.maximum(margin, 0))
    passed = jax.random.randint(jax.random.fold_in(own, 4), (count // 2,), 0, 1 << 20) % (margin + 1)
    tallies = tallies.at[donor].add(-passed).at[sink].add(passed)
    labels = jnp.searchsorted(jnp.cumsum(tallies), jnp.arange(rows * top), side="right").astype(jnp.int32)
    table = labels.reshape(top, rows).T
    table = table[jax.random.permutation(jax.random.fold_in(own, 1), rows)]
    turn = jax.random.randint(jax.random.fold_in(own, 2), (rows, 1), 0, top)
    return jnp.take_along_axis(table, (jnp.arange(top)[None, :] + turn) % top, axis=1)


def portions_of(number_of, total, bound, lean, full):
    loads = [(1 << 20) // math.isqrt(standing ** lean) + 1 for standing in range(1, number_of + 1)]
    largest = bound if full else min(bound, max(-(-total // number_of), total * loads[0] // sum(loads)))
    least = 1 if total - largest >= number_of - 1 else 0
    given, surplus = [largest] + [least] * (number_of - 1), total - largest - least * (number_of - 1)
    while surplus > 0:
        movable = [i for i in range(1, number_of) if given[i] < largest] or [i for i in range(1, number_of) if given[i] < bound]
        whole, budget = sum([loads[i] for i in movable]), surplus
        for i in movable:
            extra = min(bound - given[i], max(1, budget * loads[i] // whole), surplus)
            given[i] = given[i] + extra
            surplus = surplus - extra
    return np.array(given)


def normal_values(key, shape, scale, most, split=(), kind=jnp.bfloat16):
    values = scale * jax.random.normal(key, shape, jnp.float32)
    if split:
        values = values * shard_levels(key, shape, split, -0.22, 0.18)
    return jnp.clip(values, -most, most).astype(kind)


def setup_inputs(seed: int = 0) -> dict:
    seeds = jax.random.split(jax.random.key(seed), 14)
    positions = normal_values(seeds[0], (3, SPLATS), 1.0, 4.0, ((1, 8),), jnp.float32)
    log_scales = jnp.clip(-2.0 + 2.0 * jax.random.uniform(seeds[1], (3, SPLATS), jnp.float32) ** shard_levels(seeds[1], (3, SPLATS), ((1, 8),), -0.2, 0.2), -2.0, 0.0)
    opacity_logits = jnp.clip(-3.0 + 4.5 * jax.random.uniform(seeds[2], (1, SPLATS), jnp.float32) ** shard_levels(seeds[2], (1, SPLATS), ((1, 8),), -0.2, 0.2), -3.0, 1.5)
    colors = jnp.clip(1.0 * jax.random.uniform(seeds[3], (3, SPLATS), jnp.float32) ** shard_levels(seeds[3], (3, SPLATS), ((1, 8),), -0.2, 0.2), 0.0, 1.0)
    first_moment = normal_values(seeds[4], (10, SPLATS), 0.5, 3.0, ((1, 8),), jnp.float32)
    second_moment = jnp.clip(jnp.exp(math.log(1.0) - 4.6051702 * jax.random.uniform(seeds[5], (10, SPLATS), jnp.float32) ** shard_levels(seeds[5], (10, SPLATS), ((1, 8),), -0.2, 0.2)), 0.01, 1.0)
    cameras = jnp.clip(jax.random.uniform(seeds[6], (VIEWS, 2, 4), jnp.float32, -6.4, 6.4), -6.4, 6.4)
    background = jnp.clip(jax.random.uniform(seeds[7], (3,), jnp.float32, 0.0, 1.0), 0.0, 1.0)
    target = jnp.clip(1.0 * jax.random.uniform(seeds[8], (TILES, 3, PIX), jnp.float32) ** shard_levels(seeds[8], (TILES, 3, PIX), ((0, 8),), -0.2, 0.2), 0.0, 1.0)
    tile_view = with_ends(jax.random.randint(seeds[9], (TILES,), 0, VIEWS), jax.random.fold_in(seeds[9], 1), 0, VIEWS - 1).astype(jnp.int32)
    tile_length = with_ends(jax.random.randint(seeds[10], (TILES,), LIST // 4, LIST + 1), jax.random.fold_in(seeds[10], 1), LIST // 4, LIST).astype(jnp.int32)
    list_owner_keys = jax.random.split(jax.random.fold_in(seeds[11], 1), N_DEPTH * TILES * SLAB // (TILES_DEV * SLAB))
    list_owner_turns = jax.random.permutation(jax.random.fold_in(seeds[11], 3), N_DEPTH * TILES * SLAB // (TILES_DEV * SLAB))
    list_owner = jax.vmap(lambda own, number: deal_out(jax.random.fold_in(seeds[11], 2), own, number, TILES_DEV * SLAB, N_TILE, 1, CAP, 2))(list_owner_keys, list_owner_turns).reshape((N_DEPTH, TILES, SLAB, 1))
    list_row = with_ends(jax.random.randint(seeds[12], (N_DEPTH, TILES, SLAB), 0, G_DEV), jax.random.fold_in(seeds[12], 1), 0, G_DEV - 1).astype(jnp.int32)
    return dict(positions=positions, log_scales=log_scales, opacity_logits=opacity_logits, colors=colors, first_moment=first_moment, second_moment=second_moment, cameras=cameras, background=background, target=target, tile_view=tile_view, tile_length=tile_length, list_owner=list_owner, list_row=list_row)


def project(params, cams):
    position = params[0:3]
    variance = jnp.exp(2.0 * params[3:6])
    first_row = cams[:, 0, 0:3].T
    second_row = cams[:, 1, 0:3].T
    center_x = lax.optimization_barrier(jnp.sum(first_row * position, axis=0)) + cams[:, 0, 3] + 0.5 * TILE_SIDE
    center_y = lax.optimization_barrier(jnp.sum(second_row * position, axis=0)) + cams[:, 1, 3] + 0.5 * TILE_SIDE
    cov_xx = lax.optimization_barrier(jnp.sum(first_row * first_row * variance, axis=0)) + 0.3
    cov_xy = lax.optimization_barrier(jnp.sum(first_row * second_row * variance, axis=0))
    cov_yy = lax.optimization_barrier(jnp.sum(second_row * second_row * variance, axis=0)) + 0.3
    determinant = cov_xx * cov_yy - cov_xy * cov_xy
    return jnp.stack([center_x, center_y, cov_yy / determinant, -cov_xy / determinant, cov_xx / determinant, jax.nn.sigmoid(params[6]), params[7], params[8], params[9]])

def render_tile(screen, alive, background):
    pixel = jnp.arange(PIX, dtype=jnp.int32)
    pixel_x = (pixel % TILE_SIDE).astype(jnp.float32) + 0.5
    pixel_y = (pixel // TILE_SIDE).astype(jnp.float32) + 0.5
    offset_x = pixel_x[:, None] - screen[0][None, :]
    offset_y = pixel_y[:, None] - screen[1][None, :]
    quadric = screen[2][None, :] * offset_x * offset_x + 2.0 * screen[3][None, :] * offset_x * offset_y + screen[4][None, :] * offset_y * offset_y
    alpha = screen[5][None, :] * jnp.exp(-0.5 * quadric) * alive[None, :]
    leak = jnp.log1p(-alpha)
    before = jnp.cumsum(leak, axis=1) - leak
    weight = alpha * jnp.exp(before)
    color = jnp.einsum('ck,pk->cp', screen[6:9], weight, precision=lax.Precision.HIGHEST)
    return color + jnp.exp(lax.optimization_barrier(jnp.sum(leak, axis=1)))[None, :] * background[:, None]

def reference(positions, log_scales, opacity_logits, colors, first_moment, second_moment, cameras, background, target, tile_view, tile_length, list_owner, list_row):
    params = jnp.concatenate([positions, log_scales, opacity_logits, colors], axis=0)
    ident = (list_owner[..., 0] * G_DEV + list_row).astype(jnp.int32)
    ident = jnp.transpose(ident, (1, 0, 2)).reshape(TILES, LIST)
    live = (jnp.arange(LIST, dtype=jnp.int32)[None, :] < tile_length[:, None]).astype(jnp.float32)

    def render(values):

        def single(args):
            names, view, alive = args
            cams = jnp.broadcast_to(cameras[view], (LIST, 2, 4))
            screen = project(values[:, names], cams)
            return render_tile(screen, alive, background)
        return lax.map(jax.checkpoint(single), (ident, tile_view, live))
    image, pullback = jax.vjp(render, params)
    gradient, = pullback(image - target)
    new_first = 0.9 * first_moment + 0.1 * gradient
    new_second = 0.999 * second_moment + 0.001 * gradient * gradient
    corrected = new_first / (1.0 - 0.9 ** 10) / (jnp.sqrt(new_second / (1.0 - 0.999 ** 10)) + 1e-08)
    new_params = params - 0.05 * corrected
    return (image, new_params, new_first, new_second)
```

```python
import functools

import jax
import jax.numpy as jnp
from jax import lax
from jax.experimental import pallas as pl
from jax.experimental.pallas import tpu as pltpu
from jax.sharding import PartitionSpec as P

TILE_SIDE = 32
LANES = 128
MESH = pl.DeviceIdType.MESH
F32 = jnp.float32
BF16 = jnp.bfloat16


def exchange(items, name, ident):
    axes = []
    for _, axis, _ in items:
        if axis not in axes:
            axes.append(axis)
    sizes = {axis: lax.axis_size(axis) for axis in axes}
    count = len(items)

    def kernel(*refs):
        sources, targets = refs[:count], refs[count : 2 * count]
        sems = refs[2 * count :]
        barrier = pltpu.get_barrier_semaphore()
        for axis in axes:
            me = lax.axis_index(axis)
            for step in range(1, sizes[axis]):
                peer = lax.rem(me + step, sizes[axis])
                pl.semaphore_signal(barrier, inc=1, device_id={axis: peer}, device_id_type=MESH)
        pl.semaphore_wait(barrier, sum(sizes[axis] - 1 for axis in axes))
        copies = []
        for place, (_, axis, mode) in enumerate(items):
            source, target = sources[place], targets[place]
            send, receive, own = sems[3 * place : 3 * place + 3]
            me = lax.axis_index(axis)
            size = sizes[axis]
            for step in range(size - 1, 0, -1):
                peer = lax.rem(me + step, size)
                copy = pltpu.make_async_remote_copy(
                    src_ref=source if mode == "gather" else source.at[peer],
                    dst_ref=target.at[me],
                    send_sem=send.at[step],
                    recv_sem=receive.at[step],
                    device_id={axis: peer},
                    device_id_type=MESH,
                )
                copy.start()
                copies.append(copy)
            local = pltpu.make_async_copy(
                source if mode == "gather" else source.at[me], target.at[me], own
            )
            local.start()
            copies.append(local)
        for copy in copies:
            copy.wait()

    outs = []
    scratch = []
    for array, axis, mode in items:
        size = sizes[axis]
        shape = (size,) + (array.shape if mode == "gather" else array.shape[1:])
        outs.append(jax.ShapeDtypeStruct(shape, array.dtype))
        scratch += [
            pltpu.SemaphoreType.DMA((size,)),
            pltpu.SemaphoreType.DMA((size,)),
            pltpu.SemaphoreType.DMA,
        ]
    space = pl.BlockSpec(memory_space=pltpu.VMEM)
    return pl.pallas_call(
        kernel,
        out_shape=outs,
        in_specs=[space] * count,
        out_specs=[space] * count,
        scratch_shapes=scratch,
        name=name,
        compiler_params=pltpu.CompilerParams(
            collective_id=ident, has_side_effects=True, vmem_limit_bytes=60 << 20
        ),
    )(*[array for array, _, _ in items])


def split3(x):
    high = x.astype(BF16)
    rest = x - high.astype(F32)
    middle = rest.astype(BF16)
    low = (rest - middle.astype(F32)).astype(BF16)
    return high, middle, low


def render_kernel(
    where_ref, view_ref, length_ref, cam_ref, back_ref,
    list_ref, param_ref, target_ref,
    image_ref, grad_ref,
    picked, alphas, transes, misses, columns, sums,
):
    owners, lines = param_ref.shape[0], param_ref.shape[1]
    slabs = list_ref.shape[0]
    entries = slabs * list_ref.shape[2]
    pixels = target_ref.shape[2]
    highs = lines // 10
    chunks = pixels // LANES
    groups = entries // 8
    tile = where_ref[0]
    length = length_ref[tile]
    view = view_ref[tile]

    owner = jnp.concatenate([list_ref[d, 0:1, :] for d in range(slabs)], axis=1)
    row = jnp.concatenate([list_ref[d, 1:2, :] for d in range(slabs)], axis=1)
    low_key = row & (LANES - 1)
    high_key = owner * highs + (row >> 7)
    onehot = jnp.where(
        lax.broadcasted_iota(jnp.int32, (LANES, entries), 0) == low_key, 1.0, 0.0
    ).astype(BF16)
    twice = jnp.concatenate([onehot, onehot], axis=0)
    high_iota = lax.broadcasted_iota(jnp.int32, (highs, entries), 0)
    picked[...] = jnp.zeros_like(picked)

    def gather(o, carry):
        high, middle, low = split3(param_ref[o])
        got = jnp.dot(
            jnp.concatenate([high, middle], axis=1), twice, preferred_element_type=F32
        ) + jnp.dot(low, onehot, preferred_element_type=F32)
        mask = high_iota == high_key - o * highs
        for p in range(10):
            part = pl.ds(p * highs, highs)
            picked[part, :] = jnp.where(mask, got[p * highs : (p + 1) * highs], picked[part, :])
        return carry

    lax.fori_loop(0, owners, gather, 0, unroll=min(owners, 4))
    values = [
        jnp.sum(picked[p * highs : (p + 1) * highs, :], axis=0, keepdims=True) for p in range(10)
    ]

    base = view * 8
    first = [cam_ref[base + j] for j in range(4)]
    second = [cam_ref[base + 4 + j] for j in range(4)]
    variance = [jnp.exp(2.0 * values[3 + j]) for j in range(3)]
    half = 0.5 * TILE_SIDE
    center_x = first[0] * values[0] + first[1] * values[1] + first[2] * values[2] + first[3] + half
    center_y = second[0] * values[0] + second[1] * values[1] + second[2] * values[2] + second[3] + half
    cov_xx = sum(first[j] * first[j] * variance[j] for j in range(3)) + 0.3
    cov_xy = sum(first[j] * second[j] * variance[j] for j in range(3))
    cov_yy = sum(second[j] * second[j] * variance[j] for j in range(3)) + 0.3
    determinant = cov_xx * cov_yy - cov_xy * cov_xy
    conic_a = cov_yy / determinant
    conic_b = -cov_xy / determinant
    conic_c = cov_xx / determinant
    opacity = 1.0 / (1.0 + jnp.exp(-values[6]))
    place = lax.broadcasted_iota(jnp.int32, (1, entries), 1)
    shown = jnp.where(place < length, opacity, 0.0)
    rows = [center_x, center_y, -0.5 * conic_a, -conic_b, -0.5 * conic_c, shown] + values[7:10]
    table = jnp.concatenate(rows + [jnp.zeros((LANES - len(rows), entries), F32)], axis=0)
    columns[...] = table.T

    lane = lax.broadcasted_iota(jnp.int32, (8, LANES), 1)
    sub = lax.broadcasted_iota(jnp.int32, (8, LANES), 0)
    pixel_x = (lane & (TILE_SIDE - 1)).astype(F32) + 0.5
    pixel_y = (lane >> 5).astype(F32) + 0.5
    rows_chunk = LANES // TILE_SIDE
    ones = jnp.ones((8, LANES), F32)

    def spread(cols, j):
        return jnp.broadcast_to(cols[:, j : j + 1], (8, LANES))

    def forward(g, carry):
        trans, color = carry
        at = pl.ds(pl.multiple_of(g * 8, 8), 8)
        cols = columns[at, :]
        cx, cy, qa, qb, qc, op, red, green, blue = [spread(cols, j) for j in range(9)]
        ex = pixel_x - cx
        ey0 = pixel_y - cy
        qaxx = qa * ex * ex
        qbx = qb * ex
        new_trans, new_color = [], []
        for c in range(chunks):
            ey = ey0 + float(c * rows_chunk)
            alpha = op * jnp.exp(qaxx + (qbx + qc * ey) * ey)
            keep = 1.0 - alpha
            run = jnp.where(sub >= 1, pltpu.roll(keep, 1, 0), 1.0)
            for s in (1, 2, 4):
                run = run * jnp.where(sub >= s, pltpu.roll(run, s, 0), 1.0)
            t = run * trans[c]
            after = t * keep
            new_trans.append(jnp.broadcast_to(after[7:8, :], (8, LANES)))
            part = slice(c * LANES, (c + 1) * LANES)
            alphas[at, part] = alpha
            transes[at, part] = t
            weight = alpha * t
            new_color.append(color[3 * c] + weight * red)
            new_color.append(color[3 * c + 1] + weight * green)
            new_color.append(color[3 * c + 2] + weight * blue)
        return new_trans, new_color

    zeros = jnp.zeros((8, LANES), F32)
    trans, color = lax.fori_loop(0, groups, forward, ([ones] * chunks, [zeros] * (3 * chunks)))

    totals = []
    for c in range(chunks):
        part = slice(c * LANES, (c + 1) * LANES)
        total = 0.0
        for k in range(3):
            shade = jnp.sum(color[3 * c + k], axis=0, keepdims=True) + trans[c][0:1, :] * back_ref[k]
            image_ref[k : k + 1, part] = shade
            miss = shade - target_ref[tile, k : k + 1, part]
            misses[k, :, part] = jnp.broadcast_to(miss, (8, LANES))
            total = total + miss * shade
        totals.append(jnp.broadcast_to(total, (8, LANES)))

    def backward(g, behind):
        at = pl.ds(pl.multiple_of(g * 8, 8), 8)
        cols = columns[at, :]
        cx, cy, red, green, blue = [spread(cols, j) for j in (0, 1, 6, 7, 8)]
        ex = pixel_x - cx
        ey0 = pixel_y - cy
        new_behind = []
        acc = [zeros] * 6
        for c in range(chunks):
            part = slice(c * LANES, (c + 1) * LANES)
            alpha = alphas[at, part]
            t = transes[at, part]
            m0, m1, m2 = misses[0, :, part], misses[1, :, part], misses[2, :, part]
            weight = alpha * t
            pull = m0 * red + m1 * green + m2 * blue
            run = weight * pull
            for s in (1, 2, 4):
                run = run + jnp.where(sub >= s, pltpu.roll(run, s, 0), 0.0)
            rest = behind[c] - run
            new_behind.append(jnp.broadcast_to(rest[7:8, :], (8, LANES)))
            grad = alpha * (t * pull - rest / (1.0 - alpha))
            ey = ey0 + float(c * rows_chunk)
            gy = grad * ey
            acc[0] = acc[0] + grad
            acc[1] = acc[1] + gy
            acc[2] = acc[2] + gy * ey
            acc[3] = acc[3] + weight * m0
            acc[4] = acc[4] + weight * m1
            acc[5] = acc[5] + weight * m2
        gx = acc[0] * ex
        fields = [acc[0], gx, acc[1], gx * ex, acc[1] * ex, acc[2], acc[3], acc[4], acc[5]]
        packed = zeros
        for j, field in enumerate(fields):
            packed = jnp.where(lane == j, jnp.sum(field, axis=1, keepdims=True), packed)
        sums[at, :] = packed
        return new_behind

    lax.fori_loop(0, groups, backward, totals)

    flat = sums[...].T
    s0, sx, sy, sxx, sxy, syy, d_red, d_green, d_blue = [flat[j : j + 1, :] for j in range(9)]
    d_x = conic_a * sx + conic_b * sy
    d_y = conic_b * sx + conic_c * sy
    d_a, d_b, d_c = -0.5 * sxx, -sxy, -0.5 * syy
    d_xx = -(conic_a * conic_a * d_a + conic_a * conic_b * d_b + conic_b * conic_b * d_c)
    d_yy = -(conic_b * conic_b * d_a + conic_b * conic_c * d_b + conic_c * conic_c * d_c)
    d_xy = -(
        2.0 * conic_a * conic_b * d_a
        + (conic_a * conic_c + conic_b * conic_b) * d_b
        + 2.0 * conic_b * conic_c * d_c
    )
    out = [first[j] * d_x + second[j] * d_y for j in range(3)]
    for j in range(3):
        d_var = first[j] * first[j] * d_xx + first[j] * second[j] * d_xy + second[j] * second[j] * d_yy
        out.append(2.0 * variance[j] * d_var)
    out += [s0 * (1.0 - opacity), d_red, d_green, d_blue, owner.astype(F32), row.astype(F32)]
    out.append(jnp.zeros((16 - len(out), entries), F32))
    grad_ref[...] = jnp.concatenate(out, axis=0)


def scatter_kernel(where_ref, grads_ref, out_ref):
    sources, _, entries = grads_ref.shape
    lines = out_ref.shape[0]
    highs = lines // 10
    me = where_ref[0]
    high_iota = lax.broadcasted_iota(jnp.int32, (highs, entries), 0)
    low_iota = lax.broadcasted_iota(jnp.int32, (LANES, entries), 0)
    out_ref[...] = jnp.zeros_like(out_ref)

    def add(s, carry):
        block = grads_ref[s]
        owner = block[10:11, :].astype(jnp.int32)
        row = block[11:12, :].astype(jnp.int32)
        onehot = jnp.where(low_iota == (row & (LANES - 1)), 1.0, 0.0).astype(BF16)
        mask = high_iota == jnp.where(owner == me, row >> 7, -1)
        placed = jnp.concatenate(
            [jnp.where(mask, block[p : p + 1, :], 0.0) for p in range(10)], axis=0
        )
        high = placed.astype(BF16)
        middle = (placed - high.astype(F32)).astype(BF16)
        dims = (((1,), (1,)), ((), ()))
        out_ref[...] += lax.dot_general(
            high, onehot, dims, preferred_element_type=F32
        ) + lax.dot_general(middle, onehot, dims, preferred_element_type=F32)
        return carry

    lax.fori_loop(0, sources, add, 0, unroll=min(sources, 4))


def adam_update(param, first, second, gradient):
    new_first = 0.9 * first + 0.1 * gradient
    new_second = 0.999 * second + 0.001 * gradient * gradient
    corrected = new_first / (1.0 - 0.9**10) / (jnp.sqrt(new_second / (1.0 - 0.999**10)) + 1e-08)
    return (param - 0.05 * corrected, new_first, new_second)


def body(
    positions, log_scales, opacity_logits, colors, first_moment, second_moment,
    cameras, background, target, tile_view, tile_length, list_owner, list_row,
):
    tiles_here, _, pixels = target.shape
    slab = list_row.shape[2]
    depth_count = lax.axis_size("depth")
    entries = slab * depth_count
    here = lax.axis_index("depth").astype(jnp.int32).reshape(1)
    home = lax.axis_index("tile").astype(jnp.int32).reshape(1)
    assert tiles_here == depth_count
    params = jnp.concatenate([positions, log_scales, opacity_logits, colors], axis=0)
    splats = params.shape[1]
    lines = 10 * splats // LANES
    named = jnp.stack([list_owner[0, :, :, 0], list_row[0]], axis=1)
    every, lists = exchange(
        [(params.reshape(lines, LANES), "tile", "gather"), (named, "depth", "spread")], "share", 1
    )
    smem = pl.BlockSpec(memory_space=pltpu.SMEM)
    vmem = pl.BlockSpec(memory_space=pltpu.VMEM)
    own_image, own_grad = pl.pallas_call(
        render_kernel,
        out_shape=[
            jax.ShapeDtypeStruct((3, pixels), F32),
            jax.ShapeDtypeStruct((16, entries), F32),
        ],
        in_specs=[smem] * 5 + [vmem] * 3,
        out_specs=[vmem] * 2,
        scratch_shapes=[
            pltpu.VMEM((lines, entries), F32),
            pltpu.VMEM((entries, pixels), F32),
            pltpu.VMEM((entries, pixels), F32),
            pltpu.VMEM((3, 8, pixels), F32),
            pltpu.VMEM((entries, LANES), F32),
            pltpu.VMEM((entries, LANES), F32),
        ],
        name="render",
        compiler_params=pltpu.CompilerParams(vmem_limit_bytes=60 << 20),
    )(here, tile_view, tile_length, cameras.reshape(-1), background, lists, every, target)
    grads, image = exchange(
        [(own_grad, "tile", "gather"), (own_image, "depth", "gather")], "collect", 2
    )
    partial = pl.pallas_call(
        scatter_kernel,
        out_shape=jax.ShapeDtypeStruct((lines, LANES), F32),
        in_specs=[smem, vmem],
        out_specs=vmem,
        name="scatter",
        compiler_params=pltpu.CompilerParams(vmem_limit_bytes=60 << 20),
    )(home, grads)
    (parts,) = exchange([(partial, "depth", "gather")], "reduce", 3)
    gradient = jnp.sum(parts, axis=0).reshape(10, splats)
    new_params, new_first, new_second = adam_update(params, first_moment, second_moment, gradient)
    return (image, new_params, new_first, new_second)


def solution(mesh):
    placed = (
        P(None, "tile"),
        P(None, "tile"),
        P(None, "tile"),
        P(None, "tile"),
        P(None, "tile"),
        P(None, "tile"),
        P(),
        P(),
        P("tile", None, None),
        P("tile"),
        P("tile"),
        P("depth", "tile", None, None),
        P("depth", "tile", None),
    )
    return jax.shard_map(
        body,
        mesh=mesh,
        in_specs=placed,
        out_specs=(P("tile", None, None), P(None, "tile"), P(None, "tile"), P(None, "tile")),
        check_vma=False,
    )
```

```python
import functools

import jax
import jax.numpy as jnp
from jax import lax
from jax.experimental import pallas as pl
from jax.experimental.pallas import tpu as pltpu
from jax.sharding import PartitionSpec as P

TILE_SIDE = 32
LANES = 128
MESH = pl.DeviceIdType.MESH
F32 = jnp.float32
BF16 = jnp.bfloat16


def greet(peers):
    barrier = pltpu.get_barrier_semaphore()
    for peer in peers:
        pl.semaphore_signal(barrier, inc=1, device_id=peer, device_id_type=MESH)
    pl.semaphore_wait(barrier, len(peers))


def remote(source, target, send, receive, peer):
    return pltpu.make_async_remote_copy(
        src_ref=source, dst_ref=target, send_sem=send, recv_sem=receive,
        device_id=peer, device_id_type=MESH,
    )


def entry_rows(lists_ref, slot):
    slabs = lists_ref.shape[1]
    owner = jnp.concatenate([lists_ref[slot, d, 0:1, :] for d in range(slabs)], axis=1)
    row = jnp.concatenate([lists_ref[slot, d, 1:2, :] for d in range(slabs)], axis=1)
    return owner, row


def split3(x):
    high = x.astype(BF16)
    rest = x - high.astype(F32)
    middle = rest.astype(BF16)
    low = (rest - middle.astype(F32)).astype(BF16)
    return high, middle, low


def fetch_kernel(
    tiles, depths, named_ref, param_ref, lists_ref, entry_ref,
    high_ref, low_ref, answers, got, ask_send, ask_recv, own_sem, send, receive,
):
    lines = param_ref.shape[0]
    highs = lines // 10
    slabs, _, slab = named_ref.shape
    entries = slabs * slab
    me_t, me_d = lax.axis_index("tile"), lax.axis_index("depth")
    steps = [(a, b) for a in range(tiles - 1, -1, -1) for b in range(depths) if a or b]

    def to(a, b):
        return {"tile": lax.rem(me_t + a, tiles), "depth": lax.rem(me_d + b, depths)}

    greet([to(a, b) for a, b in steps])
    for a, b in steps:
        remote(
            named_ref.at[lax.rem(me_d + b, depths)], lists_ref.at[me_t, me_d],
            ask_send.at[a, b], ask_recv.at[a, b], to(a, b),
        ).start()
    own = pltpu.make_async_copy(named_ref.at[me_d], lists_ref.at[me_t, me_d], own_sem)
    own.start()
    high, middle, low = split3(param_ref[...])
    high_ref[...] = jnp.concatenate([high, middle], axis=1)
    low_ref[...] = low
    low_iota = lax.broadcasted_iota(jnp.int32, (LANES, entries), 0)
    high_iota = lax.broadcasted_iota(jnp.int32, (highs, entries), 0)

    def asked(a, b):
        return remote(
            named_ref.at[me_d], lists_ref.at[me_t, me_d],
            ask_send.at[a, b], ask_recv.at[a, b], to(a, b),
        )

    def answer(slot):
        owner, row = entry_rows(lists_ref, slot)
        onehot = jnp.where(low_iota == (row & (LANES - 1)), 1.0, 0.0).astype(BF16)
        twice = jnp.concatenate([onehot, onehot], axis=0)
        found = jnp.dot(high_ref[...], twice, preferred_element_type=F32) + jnp.dot(
            low_ref[...], onehot, preferred_element_type=F32
        )
        mask = high_iota == jnp.where(owner == me_t, row >> 7, -1)
        return jnp.concatenate(
            [
                jnp.sum(
                    jnp.where(mask, found[p * highs : (p + 1) * highs], 0.0), axis=0, keepdims=True
                )
                for p in range(10)
            ],
            axis=0,
        )

    def put(ref, step, rows):
        for j in range(slabs):
            ref[step, j * 10 : (j + 1) * 10, :] = rows[:, j * slab : (j + 1) * slab]

    def back(step):
        peer = {"tile": lax.rem(me_t - step + tiles, tiles)}
        return remote(answers.at[step], got.at[step], send.at[step], receive.at[step], peer)

    def serve(step, carry):
        for b in range(depths):
            asked(step, b).wait_recv()
        put(answers, step, answer(lax.rem(me_t - step + tiles, tiles)))
        back(step).start()
        return carry

    lax.fori_loop(1, tiles, serve, 0, unroll=tiles - 1 if tiles <= 8 else 1)
    own.wait()
    for b in range(1, depths):
        asked(0, b).wait_recv()
    put(got, 0, answer(me_t))
    for a, b in steps:
        asked(a, b).wait_send()
    entry_ref[...] = got[0]

    def take(step, carry):
        back(step).wait()
        entry_ref[...] += got[step]
        return carry

    lax.fori_loop(1, tiles, take, 0)


def render_kernel(
    where_ref, view_ref, length_ref, cam_ref, back_ref,
    entry_ref, target_ref,
    image_ref, grad_ref,
    alphas, transes, misses, carries, columns, sums,
):
    slabs = target_ref.shape[0]
    slab = entry_ref.shape[1]
    entries = slabs * slab
    pixels = target_ref.shape[2]
    chunks = pixels // LANES
    groups = entries // 8
    tile = where_ref[0]
    length = length_ref[tile]
    view = view_ref[tile]
    values = [
        jnp.concatenate([entry_ref[j * 10 + p : j * 10 + p + 1, :] for j in range(slabs)], axis=1)
        for p in range(10)
    ]

    base = view * 8
    first = [cam_ref[base + j] for j in range(4)]
    second = [cam_ref[base + 4 + j] for j in range(4)]
    variance = [jnp.exp(2.0 * values[3 + j]) for j in range(3)]
    half = 0.5 * TILE_SIDE
    center_x = first[0] * values[0] + first[1] * values[1] + first[2] * values[2] + first[3] + half
    center_y = second[0] * values[0] + second[1] * values[1] + second[2] * values[2] + second[3] + half
    cov_xx = sum(first[j] * first[j] * variance[j] for j in range(3)) + 0.3
    cov_xy = sum(first[j] * second[j] * variance[j] for j in range(3))
    cov_yy = sum(second[j] * second[j] * variance[j] for j in range(3)) + 0.3
    determinant = cov_xx * cov_yy - cov_xy * cov_xy
    conic_a = cov_yy / determinant
    conic_b = -cov_xy / determinant
    conic_c = cov_xx / determinant
    opacity = 1.0 / (1.0 + jnp.exp(-values[6]))
    place = lax.broadcasted_iota(jnp.int32, (1, entries), 1)
    shown = jnp.where(place < length, opacity, 0.0)
    rows = [center_x, center_y, -0.5 * conic_a, -conic_b, -0.5 * conic_c, shown] + values[7:10]
    table = jnp.concatenate(rows + [jnp.zeros((LANES - len(rows), entries), F32)], axis=0)
    columns[...] = table.T

    lane = lax.broadcasted_iota(jnp.int32, (8, LANES), 1)
    sub = lax.broadcasted_iota(jnp.int32, (8, LANES), 0)
    pixel_x = (lane & (TILE_SIDE - 1)).astype(F32) + 0.5
    pixel_y = (lane >> 5).astype(F32) + 0.5
    rows_chunk = LANES // TILE_SIDE
    ones = jnp.ones((8, LANES), F32)

    def spread(cols, j):
        return jnp.broadcast_to(cols[:, j : j + 1], (8, LANES))

    def forward(g, carry):
        trans, color = carry
        at = pl.ds(pl.multiple_of(g * 8, 8), 8)
        cols = columns[pl.ds(g, 8, stride=groups), :]
        cx, cy, qa, qb, qc, op, red, green, blue = [spread(cols, j) for j in range(9)]
        ex = pixel_x - cx
        ey0 = pixel_y - cy
        qaxx = qa * ex * ex
        qbx = qb * ex
        new_trans, new_color = [], []
        for c in range(chunks):
            ey = ey0 + float(c * rows_chunk)
            alpha = op * jnp.exp(qaxx + (qbx + qc * ey) * ey)
            t = trans[c]
            part = slice(c * LANES, (c + 1) * LANES)
            alphas[at, part] = alpha
            transes[at, part] = t
            weight = alpha * t
            new_trans.append(t - weight)
            new_color.append(color[3 * c] + weight * red)
            new_color.append(color[3 * c + 1] + weight * green)
            new_color.append(color[3 * c + 2] + weight * blue)
        return new_trans, new_color

    zeros = jnp.zeros((8, LANES), F32)
    trans, color = lax.fori_loop(
        0, groups, forward, ([ones] * chunks, [zeros] * (3 * chunks)), unroll=2
    )

    behinds = []
    for c in range(chunks):
        part = slice(c * LANES, (c + 1) * LANES)
        run = jnp.where(sub >= 1, pltpu.roll(trans[c], 1, 0), 1.0)
        for s in (1, 2, 4):
            run = run * jnp.where(sub >= s, pltpu.roll(run, s, 0), 1.0)
        carries[:, part] = run
        left = (run * trans[c])[7:8, :]
        total = 0.0
        pulled = zeros
        for k in range(3):
            lit = run * color[3 * c + k]
            shade = jnp.sum(lit, axis=0, keepdims=True) + left * back_ref[k]
            image_ref[k : k + 1, part] = shade
            miss = shade - target_ref[tile, k : k + 1, part]
            misses[k, :, part] = jnp.broadcast_to(miss, (8, LANES))
            total = total + miss * shade
            pulled = pulled + miss * lit
        ahead = jnp.where(sub >= 1, pltpu.roll(pulled, 1, 0), 0.0)
        for s in (1, 2, 4):
            ahead = ahead + jnp.where(sub >= s, pltpu.roll(ahead, s, 0), 0.0)
        behinds.append(total - ahead)

    def backward(g, behind):
        at = pl.ds(pl.multiple_of(g * 8, 8), 8)
        spaced = pl.ds(g, 8, stride=groups)
        cols = columns[spaced, :]
        cx, cy, red, green, blue = [spread(cols, j) for j in (0, 1, 6, 7, 8)]
        ex = pixel_x - cx
        ey0 = pixel_y - cy
        new_behind = []
        acc = [zeros] * 6
        for c in range(chunks):
            part = slice(c * LANES, (c + 1) * LANES)
            alpha = alphas[at, part]
            t = transes[at, part] * carries[:, part]
            m0, m1, m2 = misses[0, :, part], misses[1, :, part], misses[2, :, part]
            weight = alpha * t
            pull = m0 * red + m1 * green + m2 * blue
            rest = behind[c] - weight * pull
            new_behind.append(rest)
            grad = weight * pull - rest * (alpha / (1.0 - alpha))
            ey = ey0 + float(c * rows_chunk)
            gy = grad * ey
            acc[0] = acc[0] + grad
            acc[1] = acc[1] + gy
            acc[2] = acc[2] + gy * ey
            acc[3] = acc[3] + weight * m0
            acc[4] = acc[4] + weight * m1
            acc[5] = acc[5] + weight * m2
        gx = acc[0] * ex
        fields = [acc[0], gx, acc[1], gx * ex, acc[1] * ex, acc[2], acc[3], acc[4], acc[5]]
        packed = zeros
        for j, field in enumerate(fields):
            packed = jnp.where(lane == j, jnp.sum(field, axis=1, keepdims=True), packed)
        sums[spaced, :] = packed
        return new_behind

    lax.fori_loop(0, groups, backward, behinds, unroll=2)

    flat = sums[...].T
    s0, sx, sy, sxx, sxy, syy, d_red, d_green, d_blue = [flat[j : j + 1, :] for j in range(9)]
    d_x = conic_a * sx + conic_b * sy
    d_y = conic_b * sx + conic_c * sy
    d_a, d_b, d_c = -0.5 * sxx, -sxy, -0.5 * syy
    d_xx = -(conic_a * conic_a * d_a + conic_a * conic_b * d_b + conic_b * conic_b * d_c)
    d_yy = -(conic_b * conic_b * d_a + conic_b * conic_c * d_b + conic_c * conic_c * d_c)
    d_xy = -(
        2.0 * conic_a * conic_b * d_a
        + (conic_a * conic_c + conic_b * conic_b) * d_b
        + 2.0 * conic_b * conic_c * d_c
    )
    out = [first[j] * d_x + second[j] * d_y for j in range(3)]
    for j in range(3):
        d_var = first[j] * first[j] * d_xx + first[j] * second[j] * d_xy + second[j] * second[j] * d_yy
        out.append(2.0 * variance[j] * d_var)
    out += [s0 * (1.0 - opacity), d_red, d_green, d_blue]
    out = jnp.concatenate(out, axis=0)
    for j in range(slabs):
        grad_ref[j * 10 : (j + 1) * 10, :] = out[:, j * slab : (j + 1) * slab]


def collect_kernel(
    tiles, depths, own_ref, image_ref, lists_ref, out_ref, images_ref,
    inbox, partial, pieces, mine,
    send, receive, image_send, image_recv, image_own, cut_send, cut_recv, all_send, all_recv,
):
    lines = out_ref.shape[0]
    highs = lines // 10
    quarter = lines // depths
    slabs, slab = lists_ref.shape[1], lists_ref.shape[3]
    entries = slabs * slab
    me_t, me_d = lax.axis_index("tile"), lax.axis_index("depth")

    def along(step):
        return {"depth": lax.rem(me_d + step, depths)}

    def across(step):
        return {"tile": lax.rem(me_t + step, tiles)}

    def grads(step):
        return remote(own_ref, inbox.at[step], send.at[step], receive.at[step], across(step))

    greet([across(s) for s in range(1, tiles)] + [along(s) for s in range(1, depths)])
    for step in range(tiles - 1, 0, -1):
        grads(step).start()
    image_copies = [
        remote(image_ref, images_ref.at[me_d], image_send.at[s], image_recv.at[s], along(s))
        for s in range(1, depths)
    ]
    image_copies.append(pltpu.make_async_copy(image_ref, images_ref.at[me_d], image_own))
    for copy in image_copies:
        copy.start()

    high_iota = lax.broadcasted_iota(jnp.int32, (highs, entries), 0)
    low_iota = lax.broadcasted_iota(jnp.int32, (LANES, entries), 0)

    def placed(block, slot):
        owner, row = entry_rows(lists_ref, slot)
        onehot = jnp.where(low_iota == (row & (LANES - 1)), 1.0, 0.0).astype(BF16)
        mask = high_iota == jnp.where(owner == me_t, row >> 7, -1)
        wide = jnp.concatenate([block[j * 10 : (j + 1) * 10, :] for j in range(slabs)], axis=1)
        spots = jnp.concatenate(
            [jnp.where(mask, wide[p : p + 1, :], 0.0) for p in range(10)], axis=0
        )
        high = spots.astype(BF16)
        middle = (spots - high.astype(F32)).astype(BF16)
        dims = (((1,), (1,)), ((), ()))
        return lax.dot_general(
            high, onehot, dims, preferred_element_type=F32
        ) + lax.dot_general(middle, onehot, dims, preferred_element_type=F32)

    partial[...] = placed(own_ref[...], me_t)

    def add(step, carry):
        grads(step).wait()
        partial[...] += placed(inbox[step], lax.rem(me_t - step + tiles, tiles))
        return carry

    lax.fori_loop(1, tiles, add, 0, unroll=tiles - 1 if tiles <= 8 else 1)
    for copy in image_copies:
        copy.wait()

    def rows_of(index):
        return pl.ds(pl.multiple_of(index * quarter, 8), quarter)

    cuts = [
        remote(
            partial.at[rows_of(lax.rem(me_d + s, depths))], pieces.at[s],
            cut_send.at[s], cut_recv.at[s], along(s),
        )
        for s in range(1, depths)
    ]
    for copy in cuts:
        copy.start()
    total = partial[rows_of(me_d), :]
    for s, copy in enumerate(cuts):
        copy.wait()
        total = total + pieces[s + 1]
    mine[...] = total
    shares = [
        remote(mine, out_ref.at[rows_of(me_d)], all_send.at[s], all_recv.at[s], along(s))
        for s in range(1, depths)
    ]
    for copy in shares:
        copy.start()
    out_ref[rows_of(me_d), :] = total
    for copy in shares:
        copy.wait()


def adam_update(param, first, second, gradient):
    new_first = 0.9 * first + 0.1 * gradient
    new_second = 0.999 * second + 0.001 * gradient * gradient
    corrected = new_first / (1.0 - 0.9**10) / (jnp.sqrt(new_second / (1.0 - 0.999**10)) + 1e-08)
    return (param - 0.05 * corrected, new_first, new_second)


def body(
    positions, log_scales, opacity_logits, colors, first_moment, second_moment,
    cameras, background, target, tile_view, tile_length, list_owner, list_row,
):
    tiles_here, _, pixels = target.shape
    slab = list_row.shape[2]
    depth_count = lax.axis_size("depth")
    entries = slab * depth_count
    here = lax.axis_index("depth").astype(jnp.int32).reshape(1)
    assert tiles_here == depth_count
    params = jnp.concatenate([positions, log_scales, opacity_logits, colors], axis=0)
    splats = params.shape[1]
    lines = 10 * splats // LANES
    named = jnp.stack([list_owner[0, :, :, 0], list_row[0]], axis=1)
    tile_count = lax.axis_size("tile")
    assert 10 * slab * depth_count % LANES == 0 and slab == LANES
    smem = pl.BlockSpec(memory_space=pltpu.SMEM)
    vmem = pl.BlockSpec(memory_space=pltpu.VMEM)
    dma = pltpu.SemaphoreType.DMA
    block = (10 * depth_count, slab)
    limit = 60 << 20
    lists, entry = pl.pallas_call(
        functools.partial(fetch_kernel, tile_count, depth_count),
        out_shape=[
            jax.ShapeDtypeStruct((tile_count, depth_count, 2, slab), jnp.int32),
            jax.ShapeDtypeStruct(block, F32),
        ],
        in_specs=[vmem] * 2,
        out_specs=[vmem] * 2,
        scratch_shapes=[
            pltpu.VMEM((lines, 2 * LANES), BF16),
            pltpu.VMEM((lines, LANES), BF16),
            pltpu.VMEM((tile_count,) + block, F32),
            pltpu.VMEM((tile_count,) + block, F32),
            dma((tile_count, depth_count)),
            dma((tile_count, depth_count)),
            dma,
            dma((tile_count,)),
            dma((tile_count,)),
        ],
        name="fetch",
        compiler_params=pltpu.CompilerParams(
            collective_id=1, has_side_effects=True, vmem_limit_bytes=limit
        ),
    )(named, params.reshape(lines, LANES))
    own_image, own_grad = pl.pallas_call(
        render_kernel,
        out_shape=[
            jax.ShapeDtypeStruct((3, pixels), F32),
            jax.ShapeDtypeStruct(block, F32),
        ],
        in_specs=[smem] * 5 + [vmem] * 2,
        out_specs=[vmem] * 2,
        scratch_shapes=[
            pltpu.VMEM((entries, pixels), F32),
            pltpu.VMEM((entries, pixels), F32),
            pltpu.VMEM((3, 8, pixels), F32),
            pltpu.VMEM((8, pixels), F32),
            pltpu.VMEM((entries, LANES), F32),
            pltpu.VMEM((entries, LANES), F32),
        ],
        name="render",
        compiler_params=pltpu.CompilerParams(vmem_limit_bytes=limit),
    )(here, tile_view, tile_length, cameras.reshape(-1), background, entry, target)
    quarter = lines // depth_count
    total, image = pl.pallas_call(
        functools.partial(collect_kernel, tile_count, depth_count),
        out_shape=[
            jax.ShapeDtypeStruct((lines, LANES), F32),
            jax.ShapeDtypeStruct((depth_count, 3, pixels), F32),
        ],
        in_specs=[vmem] * 3,
        out_specs=[vmem] * 2,
        scratch_shapes=[
            pltpu.VMEM((tile_count,) + block, F32),
            pltpu.VMEM((lines, LANES), F32),
            pltpu.VMEM((depth_count, quarter, LANES), F32),
            pltpu.VMEM((quarter, LANES), F32),
            dma((tile_count,)),
            dma((tile_count,)),
            dma((depth_count,)),
            dma((depth_count,)),
            dma,
            dma((depth_count,)),
            dma((depth_count,)),
            dma((depth_count,)),
            dma((depth_count,)),
        ],
        name="collect",
        compiler_params=pltpu.CompilerParams(
            collective_id=2, has_side_effects=True, vmem_limit_bytes=limit
        ),
    )(own_grad, own_image, lists)
    gradient = total.reshape(10, splats)
    new_params, new_first, new_second = adam_update(params, first_moment, second_moment, gradient)
    return (image, new_params, new_first, new_second)


def solution(mesh):
    placed = (
        P(None, "tile"),
        P(None, "tile"),
        P(None, "tile"),
        P(None, "tile"),
        P(None, "tile"),
        P(None, "tile"),
        P(),
        P(),
        P("tile", None, None),
        P("tile"),
        P("tile"),
        P("depth", "tile", None, None),
        P("depth", "tile", None),
    )
    return jax.shard_map(
        body,
        mesh=mesh,
        in_specs=placed,
        out_specs=(P("tile", None, None), P(None, "tile"), P(None, "tile"), P(None, "tile")),
        check_vma=False,
    )
```

```python
import functools

import jax
import jax.numpy as jnp
from jax import lax
from jax.experimental import pallas as pl
from jax.experimental.pallas import tpu as pltpu
from jax.sharding import PartitionSpec as P

TILE_SIDE = 32
LANES = 128
MESH = pl.DeviceIdType.MESH
F32 = jnp.float32
BF16 = jnp.bfloat16


def greet(peers):
    barrier = pltpu.get_barrier_semaphore()
    for peer in peers:
        pl.semaphore_signal(barrier, inc=1, device_id=peer, device_id_type=MESH)
    pl.semaphore_wait(barrier, len(peers))


def remote(source, target, send, receive, peer):
    return pltpu.make_async_remote_copy(
        src_ref=source, dst_ref=target, send_sem=send, recv_sem=receive,
        device_id=peer, device_id_type=MESH,
    )


def entry_rows(lists_ref, slot):
    slabs = lists_ref.shape[1]
    owner = jnp.concatenate([lists_ref[slot, d, 0:1, :] for d in range(slabs)], axis=1)
    row = jnp.concatenate([lists_ref[slot, d, 1:2, :] for d in range(slabs)], axis=1)
    return owner, row


def split3(x):
    high = x.astype(BF16)
    rest = x - high.astype(F32)
    middle = rest.astype(BF16)
    low = (rest - middle.astype(F32)).astype(BF16)
    return high, middle, low


def fetch_kernel(
    tiles, depths, owner_ref, row_ref, place_ref, scale_ref, logit_ref, color_ref,
    lists_ref, entry_ref,
    named_ref, param_ref, high_ref, low_ref, answers, got, ask_send, ask_recv, own_sem, send, receive,
):
    lines = param_ref.shape[0]
    highs = lines // 10
    slabs, _, slab = named_ref.shape
    entries = slabs * slab
    for q in range(slabs):
        named_ref[q, 0:1, :] = owner_ref[q]
        named_ref[q, 1:2, :] = row_ref[q : q + 1, :]
    param = 0
    for ref in (place_ref, scale_ref, logit_ref, color_ref):
        for k in range(ref.shape[0]):
            for h in range(highs):
                line = param * highs + h
                param_ref[line : line + 1, :] = ref[k : k + 1, h * LANES : (h + 1) * LANES]
            param += 1
    me_t, me_d = lax.axis_index("tile"), lax.axis_index("depth")
    steps = [(a, b) for a in range(tiles - 1, -1, -1) for b in range(depths) if a or b]

    def to(a, b):
        return {"tile": lax.rem(me_t + a, tiles), "depth": lax.rem(me_d + b, depths)}

    greet([to(a, b) for a, b in steps])
    for a, b in steps:
        remote(
            named_ref.at[lax.rem(me_d + b, depths)], lists_ref.at[me_t, me_d],
            ask_send.at[a, b], ask_recv.at[a, b], to(a, b),
        ).start()
    own = pltpu.make_async_copy(named_ref.at[me_d], lists_ref.at[me_t, me_d], own_sem)
    own.start()
    high, middle, low = split3(param_ref[...])
    high_ref[...] = jnp.concatenate([high, middle], axis=1)
    low_ref[...] = low
    low_iota = lax.broadcasted_iota(jnp.int32, (LANES, entries), 0)
    high_iota = lax.broadcasted_iota(jnp.int32, (highs, entries), 0)

    def asked(a, b):
        return remote(
            named_ref.at[me_d], lists_ref.at[me_t, me_d],
            ask_send.at[a, b], ask_recv.at[a, b], to(a, b),
        )

    def answer(slot):
        owner, row = entry_rows(lists_ref, slot)
        onehot = jnp.where(low_iota == (row & (LANES - 1)), 1.0, 0.0).astype(BF16)
        twice = jnp.concatenate([onehot, onehot], axis=0)
        found = jnp.dot(high_ref[...], twice, preferred_element_type=F32) + jnp.dot(
            low_ref[...], onehot, preferred_element_type=F32
        )
        mask = high_iota == jnp.where(owner == me_t, row >> 7, -1)
        return jnp.concatenate(
            [
                jnp.sum(
                    jnp.where(mask, found[p * highs : (p + 1) * highs], 0.0), axis=0, keepdims=True
                )
                for p in range(10)
            ],
            axis=0,
        )

    def put(ref, step, rows):
        for j in range(slabs):
            ref[step, j * 10 : (j + 1) * 10, :] = rows[:, j * slab : (j + 1) * slab]

    def back(step):
        peer = {"tile": lax.rem(me_t - step + tiles, tiles)}
        return remote(answers.at[step], got.at[step], send.at[step], receive.at[step], peer)

    def serve(step, carry):
        for b in range(depths):
            asked(step, b).wait_recv()
        put(answers, step, answer(lax.rem(me_t - step + tiles, tiles)))
        back(step).start()
        return carry

    lax.fori_loop(1, tiles, serve, 0, unroll=tiles - 1 if tiles <= 8 else 1)
    own.wait()
    for b in range(1, depths):
        asked(0, b).wait_recv()
    put(got, 0, answer(me_t))
    for a, b in steps:
        asked(a, b).wait_send()
    entry_ref[...] = got[0]

    def take(step, carry):
        back(step).wait()
        entry_ref[...] += got[step]
        return carry

    lax.fori_loop(1, tiles, take, 0)


def render_kernel(
    where_ref, view_ref, length_ref, cam_ref, back_ref,
    entry_ref, target_ref,
    image_ref, grad_ref,
    alphas, transes, misses, carries, columns, sums,
):
    slabs = target_ref.shape[1]
    slab = entry_ref.shape[1]
    entries = slabs * slab
    pixels = target_ref.shape[2]
    chunks = pixels // LANES
    groups = entries // 8
    tile = where_ref[0]
    length = length_ref[tile]
    view = view_ref[tile]
    values = [
        jnp.concatenate([entry_ref[j * 10 + p : j * 10 + p + 1, :] for j in range(slabs)], axis=1)
        for p in range(10)
    ]

    first = [cam_ref[view, 0, j] for j in range(4)]
    second = [cam_ref[view, 1, j] for j in range(4)]
    variance = [jnp.exp(2.0 * values[3 + j]) for j in range(3)]
    half = 0.5 * TILE_SIDE
    center_x = first[0] * values[0] + first[1] * values[1] + first[2] * values[2] + first[3] + half
    center_y = second[0] * values[0] + second[1] * values[1] + second[2] * values[2] + second[3] + half
    cov_xx = sum(first[j] * first[j] * variance[j] for j in range(3)) + 0.3
    cov_xy = sum(first[j] * second[j] * variance[j] for j in range(3))
    cov_yy = sum(second[j] * second[j] * variance[j] for j in range(3)) + 0.3
    determinant = cov_xx * cov_yy - cov_xy * cov_xy
    conic_a = cov_yy / determinant
    conic_b = -cov_xy / determinant
    conic_c = cov_xx / determinant
    opacity = 1.0 / (1.0 + jnp.exp(-values[6]))
    place = lax.broadcasted_iota(jnp.int32, (1, entries), 1)
    shown = jnp.where(place < length, opacity, 0.0)
    rows = [center_x, center_y, -0.5 * conic_a, -conic_b, -0.5 * conic_c, shown] + values[7:10]
    table = jnp.concatenate(rows + [jnp.zeros((LANES - len(rows), entries), F32)], axis=0)
    columns[...] = table.T

    lane = lax.broadcasted_iota(jnp.int32, (8, LANES), 1)
    sub = lax.broadcasted_iota(jnp.int32, (8, LANES), 0)
    pixel_x = (lane & (TILE_SIDE - 1)).astype(F32) + 0.5
    pixel_y = (lane >> 5).astype(F32) + 0.5
    rows_chunk = LANES // TILE_SIDE
    ones = jnp.ones((8, LANES), F32)

    def spread(cols, j):
        return jnp.broadcast_to(cols[:, j : j + 1], (8, LANES))

    def forward(g, carry):
        trans, color = carry
        at = pl.ds(pl.multiple_of(g * 8, 8), 8)
        cols = columns[pl.ds(g, 8, stride=groups), :]
        cx, cy, qa, qb, qc, op, red, green, blue = [spread(cols, j) for j in range(9)]
        ex = pixel_x - cx
        ey0 = pixel_y - cy
        qaxx = qa * ex * ex
        qbx = qb * ex
        new_trans, new_color = [], []
        for c in range(chunks):
            ey = ey0 + float(c * rows_chunk)
            alpha = op * jnp.exp(qaxx + (qbx + qc * ey) * ey)
            t = trans[c]
            part = slice(c * LANES, (c + 1) * LANES)
            alphas[at, part] = alpha
            transes[at, part] = t
            weight = alpha * t
            new_trans.append(t - weight)
            new_color.append(color[3 * c] + weight * red)
            new_color.append(color[3 * c + 1] + weight * green)
            new_color.append(color[3 * c + 2] + weight * blue)
        return new_trans, new_color

    zeros = jnp.zeros((8, LANES), F32)
    trans, color = lax.fori_loop(
        0, groups, forward, ([ones] * chunks, [zeros] * (3 * chunks)), unroll=2
    )

    chosen = lax.broadcasted_iota(jnp.int32, (slabs, LANES), 0) == tile
    behinds = []
    for c in range(chunks):
        part = slice(c * LANES, (c + 1) * LANES)
        run = jnp.where(sub >= 1, pltpu.roll(trans[c], 1, 0), 1.0)
        for s in (1, 2, 4):
            run = run * jnp.where(sub >= s, pltpu.roll(run, s, 0), 1.0)
        carries[:, part] = run
        left = (run * trans[c])[7:8, :]
        total = 0.0
        pulled = zeros
        for k in range(3):
            lit = run * color[3 * c + k]
            shade = jnp.sum(lit, axis=0, keepdims=True) + left * back_ref[k]
            image_ref[k : k + 1, part] = shade
            miss = shade - jnp.sum(
                jnp.where(chosen, target_ref[k, :, part], 0.0), axis=0, keepdims=True
            )
            misses[k, :, part] = jnp.broadcast_to(miss, (8, LANES))
            total = total + miss * shade
            pulled = pulled + miss * lit
        ahead = jnp.where(sub >= 1, pltpu.roll(pulled, 1, 0), 0.0)
        for s in (1, 2, 4):
            ahead = ahead + jnp.where(sub >= s, pltpu.roll(ahead, s, 0), 0.0)
        behinds.append(total - ahead)

    def backward(g, behind):
        at = pl.ds(pl.multiple_of(g * 8, 8), 8)
        spaced = pl.ds(g, 8, stride=groups)
        cols = columns[spaced, :]
        cx, cy, red, green, blue = [spread(cols, j) for j in (0, 1, 6, 7, 8)]
        ex = pixel_x - cx
        ey0 = pixel_y - cy
        new_behind = []
        acc = [zeros] * 6
        for c in range(chunks):
            part = slice(c * LANES, (c + 1) * LANES)
            alpha = alphas[at, part]
            t = transes[at, part] * carries[:, part]
            m0, m1, m2 = misses[0, :, part], misses[1, :, part], misses[2, :, part]
            weight = alpha * t
            pull = m0 * red + m1 * green + m2 * blue
            rest = behind[c] - weight * pull
            new_behind.append(rest)
            grad = weight * pull - rest * (alpha / (1.0 - alpha))
            ey = ey0 + float(c * rows_chunk)
            gy = grad * ey
            acc[0] = acc[0] + grad
            acc[1] = acc[1] + gy
            acc[2] = acc[2] + gy * ey
            acc[3] = acc[3] + weight * m0
            acc[4] = acc[4] + weight * m1
            acc[5] = acc[5] + weight * m2
        gx = acc[0] * ex
        fields = [acc[0], gx, acc[1], gx * ex, acc[1] * ex, acc[2], acc[3], acc[4], acc[5]]
        packed = zeros
        for j, field in enumerate(fields):
            packed = jnp.where(lane == j, jnp.sum(field, axis=1, keepdims=True), packed)
        sums[spaced, :] = packed
        return new_behind

    lax.fori_loop(0, groups, backward, behinds, unroll=2)

    flat = sums[...].T
    s0, sx, sy, sxx, sxy, syy, d_red, d_green, d_blue = [flat[j : j + 1, :] for j in range(9)]
    d_x = conic_a * sx + conic_b * sy
    d_y = conic_b * sx + conic_c * sy
    d_a, d_b, d_c = -0.5 * sxx, -sxy, -0.5 * syy
    d_xx = -(conic_a * conic_a * d_a + conic_a * conic_b * d_b + conic_b * conic_b * d_c)
    d_yy = -(conic_b * conic_b * d_a + conic_b * conic_c * d_b + conic_c * conic_c * d_c)
    d_xy = -(
        2.0 * conic_a * conic_b * d_a
        + (conic_a * conic_c + conic_b * conic_b) * d_b
        + 2.0 * conic_b * conic_c * d_c
    )
    out = [first[j] * d_x + second[j] * d_y for j in range(3)]
    for j in range(3):
        d_var = first[j] * first[j] * d_xx + first[j] * second[j] * d_xy + second[j] * second[j] * d_yy
        out.append(2.0 * variance[j] * d_var)
    out += [s0 * (1.0 - opacity), d_red, d_green, d_blue]
    out = jnp.concatenate(out, axis=0)
    for j in range(slabs):
        grad_ref[j * 10 : (j + 1) * 10, :] = out[:, j * slab : (j + 1) * slab]


def collect_kernel(
    tiles, depths, own_ref, image_ref, lists_ref, gradient_ref, picture_ref,
    images_ref, out_ref, inbox, partial, pieces, mine,
    send, receive, image_send, image_recv, image_own, cut_send, cut_recv, all_send, all_recv,
):
    lines = out_ref.shape[0]
    highs = lines // 10
    quarter = lines // depths
    slabs, slab = lists_ref.shape[1], lists_ref.shape[3]
    entries = slabs * slab
    me_t, me_d = lax.axis_index("tile"), lax.axis_index("depth")

    def along(step):
        return {"depth": lax.rem(me_d + step, depths)}

    def across(step):
        return {"tile": lax.rem(me_t + step, tiles)}

    def grads(step):
        return remote(own_ref, inbox.at[step], send.at[step], receive.at[step], across(step))

    greet([across(s) for s in range(1, tiles)] + [along(s) for s in range(1, depths)])
    for step in range(tiles - 1, 0, -1):
        grads(step).start()
    image_copies = [
        remote(image_ref, images_ref.at[me_d], image_send.at[s], image_recv.at[s], along(s))
        for s in range(1, depths)
    ]
    image_copies.append(pltpu.make_async_copy(image_ref, images_ref.at[me_d], image_own))
    for copy in image_copies:
        copy.start()

    high_iota = lax.broadcasted_iota(jnp.int32, (highs, entries), 0)
    low_iota = lax.broadcasted_iota(jnp.int32, (LANES, entries), 0)

    def placed(block, slot):
        owner, row = entry_rows(lists_ref, slot)
        onehot = jnp.where(low_iota == (row & (LANES - 1)), 1.0, 0.0).astype(BF16)
        mask = high_iota == jnp.where(owner == me_t, row >> 7, -1)
        wide = jnp.concatenate([block[j * 10 : (j + 1) * 10, :] for j in range(slabs)], axis=1)
        spots = jnp.concatenate(
            [jnp.where(mask, wide[p : p + 1, :], 0.0) for p in range(10)], axis=0
        )
        high = spots.astype(BF16)
        middle = (spots - high.astype(F32)).astype(BF16)
        dims = (((1,), (1,)), ((), ()))
        return lax.dot_general(
            high, onehot, dims, preferred_element_type=F32
        ) + lax.dot_general(middle, onehot, dims, preferred_element_type=F32)

    partial[...] = placed(own_ref[...], me_t)

    def add(step, carry):
        grads(step).wait()
        partial[...] += placed(inbox[step], lax.rem(me_t - step + tiles, tiles))
        return carry

    lax.fori_loop(1, tiles, add, 0, unroll=tiles - 1 if tiles <= 8 else 1)
    for copy in image_copies:
        copy.wait()

    def rows_of(index):
        return pl.ds(pl.multiple_of(index * quarter, 8), quarter)

    cuts = [
        remote(
            partial.at[rows_of(lax.rem(me_d + s, depths))], pieces.at[s],
            cut_send.at[s], cut_recv.at[s], along(s),
        )
        for s in range(1, depths)
    ]
    for copy in cuts:
        copy.start()
    total = partial[rows_of(me_d), :]
    for s, copy in enumerate(cuts):
        copy.wait()
        total = total + pieces[s + 1]
    mine[...] = total
    shares = [
        remote(mine, out_ref.at[rows_of(me_d)], all_send.at[s], all_recv.at[s], along(s))
        for s in range(1, depths)
    ]
    for copy in shares:
        copy.start()
    out_ref[rows_of(me_d), :] = total
    for d in range(depths):
        for k in range(3):
            picture_ref[k, d : d + 1, :] = images_ref[d, k : k + 1, :]
    for copy in shares:
        copy.wait()
    for p in range(10):
        for h in range(highs):
            line = p * highs + h
            gradient_ref[p : p + 1, h * LANES : (h + 1) * LANES] = out_ref[line : line + 1, :]


def adam_update(param, first, second, gradient):
    new_first = 0.9 * first + 0.1 * gradient
    new_second = 0.999 * second + 0.001 * gradient * gradient
    corrected = new_first / (1.0 - 0.9**10) / (jnp.sqrt(new_second / (1.0 - 0.999**10)) + 1e-08)
    return (param - 0.05 * corrected, new_first, new_second)


def body(
    positions, log_scales, opacity_logits, colors, first_moment, second_moment,
    cameras, background, target, tile_view, tile_length, list_owner, list_row,
):
    tiles_here, _, pixels = target.shape
    slab = list_row.shape[2]
    depth_count = lax.axis_size("depth")
    entries = slab * depth_count
    here = lax.axis_index("depth").astype(jnp.int32).reshape(1)
    assert tiles_here == depth_count
    params = jnp.concatenate([positions, log_scales, opacity_logits, colors], axis=0)
    splats = params.shape[1]
    lines = 10 * splats // LANES
    tile_count = lax.axis_size("tile")
    assert 10 * slab * depth_count % LANES == 0 and slab == LANES
    smem = pl.BlockSpec(memory_space=pltpu.SMEM)
    vmem = pl.BlockSpec(memory_space=pltpu.VMEM)
    dma = pltpu.SemaphoreType.DMA
    block = (10 * depth_count, slab)
    limit = 60 << 20
    lists, entry = pl.pallas_call(
        functools.partial(fetch_kernel, tile_count, depth_count),
        out_shape=[
            jax.ShapeDtypeStruct((tile_count, depth_count, 2, slab), jnp.int32),
            jax.ShapeDtypeStruct(block, F32),
        ],
        in_specs=[vmem] * 6,
        out_specs=[vmem] * 2,
        scratch_shapes=[
            pltpu.VMEM((depth_count, 2, slab), jnp.int32),
            pltpu.VMEM((lines, LANES), F32),
            pltpu.VMEM((lines, 2 * LANES), BF16),
            pltpu.VMEM((lines, LANES), BF16),
            pltpu.VMEM((tile_count,) + block, F32),
            pltpu.VMEM((tile_count,) + block, F32),
            dma((tile_count, depth_count)),
            dma((tile_count, depth_count)),
            dma,
            dma((tile_count,)),
            dma((tile_count,)),
        ],
        name="fetch",
        compiler_params=pltpu.CompilerParams(
            collective_id=1, has_side_effects=True, vmem_limit_bytes=limit
        ),
    )(
        list_owner.reshape(tiles_here, 1, slab), list_row[0],
        positions, log_scales, opacity_logits, colors,
    )
    own_image, own_grad = pl.pallas_call(
        render_kernel,
        out_shape=[
            jax.ShapeDtypeStruct((3, pixels), F32),
            jax.ShapeDtypeStruct(block, F32),
        ],
        in_specs=[smem] * 5 + [vmem] * 2,
        out_specs=[vmem] * 2,
        scratch_shapes=[
            pltpu.VMEM((entries, pixels), F32),
            pltpu.VMEM((entries, pixels), F32),
            pltpu.VMEM((3, 8, pixels), F32),
            pltpu.VMEM((8, pixels), F32),
            pltpu.VMEM((entries, LANES), F32),
            pltpu.VMEM((entries, LANES), F32),
        ],
        name="render",
        compiler_params=pltpu.CompilerParams(vmem_limit_bytes=limit),
    )(here, tile_view, tile_length, cameras, background, entry, target.transpose(1, 0, 2))
    quarter = lines // depth_count
    gradient, picture = pl.pallas_call(
        functools.partial(collect_kernel, tile_count, depth_count),
        out_shape=[
            jax.ShapeDtypeStruct((10, splats), F32),
            jax.ShapeDtypeStruct((3, depth_count, pixels), F32),
        ],
        in_specs=[vmem] * 3,
        out_specs=[vmem] * 2,
        scratch_shapes=[
            pltpu.VMEM((depth_count, 3, pixels), F32),
            pltpu.VMEM((lines, LANES), F32),
            pltpu.VMEM((tile_count,) + block, F32),
            pltpu.VMEM((lines, LANES), F32),
            pltpu.VMEM((depth_count, quarter, LANES), F32),
            pltpu.VMEM((quarter, LANES), F32),
            dma((tile_count,)),
            dma((tile_count,)),
            dma((depth_count,)),
            dma((depth_count,)),
            dma,
            dma((depth_count,)),
            dma((depth_count,)),
            dma((depth_count,)),
            dma((depth_count,)),
        ],
        name="collect",
        compiler_params=pltpu.CompilerParams(
            collective_id=2, has_side_effects=True, vmem_limit_bytes=limit
        ),
    )(own_grad, own_image, lists)
    image = picture.transpose(1, 0, 2)
    new_params, new_first, new_second = adam_update(params, first_moment, second_moment, gradient)
    return (image, new_params, new_first, new_second)


def solution(mesh):
    placed = (
        P(None, "tile"),
        P(None, "tile"),
        P(None, "tile"),
        P(None, "tile"),
        P(None, "tile"),
        P(None, "tile"),
        P(),
        P(),
        P("tile", None, None),
        P("tile"),
        P("tile"),
        P("depth", "tile", None, None),
        P("depth", "tile", None),
    )
    return jax.shard_map(
        body,
        mesh=mesh,
        in_specs=placed,
        out_specs=(P("tile", None, None), P(None, "tile"), P(None, "tile"), P(None, "tile")),
        check_vma=False,
    )
```

```python
import functools

import jax
import jax.numpy as jnp
from jax import lax
from jax.experimental import pallas as pl
from jax.experimental.pallas import tpu as pltpu
from jax.sharding import PartitionSpec as P

TILE_SIDE = 32
LANES = 128
MESH = pl.DeviceIdType.MESH
F32 = jnp.float32
BF16 = jnp.bfloat16


def greet(peers):
    barrier = pltpu.get_barrier_semaphore()
    for peer in peers:
        pl.semaphore_signal(barrier, inc=1, device_id=peer, device_id_type=MESH)
    pl.semaphore_wait(barrier, len(peers))


def remote(source, target, send, receive, peer):
    return pltpu.make_async_remote_copy(
        src_ref=source, dst_ref=target, send_sem=send, recv_sem=receive,
        device_id=peer, device_id_type=MESH,
    )


def entry_rows(lists_ref, slot):
    slabs = lists_ref.shape[1]
    owner = jnp.concatenate([lists_ref[slot, d, 0:1, :] for d in range(slabs)], axis=1)
    row = jnp.concatenate([lists_ref[slot, d, 1:2, :] for d in range(slabs)], axis=1)
    return owner, row


def split3(x):
    high = x.astype(BF16)
    rest = x - high.astype(F32)
    middle = rest.astype(BF16)
    low = (rest - middle.astype(F32)).astype(BF16)
    return high, middle, low


def fetch_kernel(
    tiles, depths, owner_ref, row_ref, place_ref, scale_ref, logit_ref, color_ref,
    lists_ref, entry_ref,
    named_ref, param_ref, high_ref, low_ref, answers, got, ask_send, ask_recv, own_sem, send, receive,
):
    lines = param_ref.shape[0]
    highs = lines // 10
    slabs, _, slab = named_ref.shape
    entries = slabs * slab
    for q in range(slabs):
        named_ref[q, 0:1, :] = owner_ref[q]
        named_ref[q, 1:2, :] = row_ref[q : q + 1, :]
    param = 0
    for ref in (place_ref, scale_ref, logit_ref, color_ref):
        for k in range(ref.shape[0]):
            for h in range(highs):
                line = param * highs + h
                param_ref[line : line + 1, :] = ref[k : k + 1, h * LANES : (h + 1) * LANES]
            param += 1
    me_t, me_d = lax.axis_index("tile"), lax.axis_index("depth")
    steps = [(a, b) for a in range(tiles - 1, -1, -1) for b in range(depths) if a or b]

    def to(a, b):
        return {"tile": lax.rem(me_t + a, tiles), "depth": lax.rem(me_d + b, depths)}

    greet([to(a, b) for a, b in steps])
    for a, b in steps:
        remote(
            named_ref.at[lax.rem(me_d + b, depths)], lists_ref.at[me_t, me_d],
            ask_send.at[a, b], ask_recv.at[a, b], to(a, b),
        ).start()
    own = pltpu.make_async_copy(named_ref.at[me_d], lists_ref.at[me_t, me_d], own_sem)
    own.start()
    high, middle, low = split3(param_ref[...])
    high_ref[...] = jnp.concatenate([high, middle], axis=1)
    low_ref[...] = low
    low_iota = lax.broadcasted_iota(jnp.int32, (LANES, entries), 0)
    high_iota = lax.broadcasted_iota(jnp.int32, (highs, entries), 0)

    def asked(a, b):
        return remote(
            named_ref.at[me_d], lists_ref.at[me_t, me_d],
            ask_send.at[a, b], ask_recv.at[a, b], to(a, b),
        )

    def answer(slot):
        owner, row = entry_rows(lists_ref, slot)
        onehot = jnp.where(low_iota == (row & (LANES - 1)), 1.0, 0.0).astype(BF16)
        twice = jnp.concatenate([onehot, onehot], axis=0)
        found = jnp.dot(high_ref[...], twice, preferred_element_type=F32) + jnp.dot(
            low_ref[...], onehot, preferred_element_type=F32
        )
        mask = high_iota == jnp.where(owner == me_t, row >> 7, -1)
        return jnp.concatenate(
            [
                jnp.sum(
                    jnp.where(mask, found[p * highs : (p + 1) * highs], 0.0), axis=0, keepdims=True
                )
                for p in range(10)
            ],
            axis=0,
        )

    def put(ref, step, rows):
        for j in range(slabs):
            ref[step, j * 10 : (j + 1) * 10, :] = rows[:, j * slab : (j + 1) * slab]

    def back(step):
        peer = {"tile": lax.rem(me_t - step + tiles, tiles)}
        return remote(answers.at[step], got.at[step], send.at[step], receive.at[step], peer)

    def serve(step, carry):
        for b in range(depths):
            asked(step, b).wait_recv()
        put(answers, step, answer(lax.rem(me_t - step + tiles, tiles)))
        back(step).start()
        return carry

    lax.fori_loop(1, tiles, serve, 0, unroll=tiles - 1 if tiles <= 8 else 1)
    own.wait()
    for b in range(1, depths):
        asked(0, b).wait_recv()
    put(got, 0, answer(me_t))
    for a, b in steps:
        asked(a, b).wait_send()
    entry_ref[...] = got[0]

    def take(step, carry):
        back(step).wait()
        entry_ref[...] += got[step]
        return carry

    lax.fori_loop(1, tiles, take, 0)


def render_kernel(
    where_ref, view_ref, length_ref, cam_ref, back_ref,
    entry_ref, target_ref,
    image_ref, grad_ref,
    alphas, weights, misses, carries, columns, sums,
):
    slabs = target_ref.shape[1]
    slab = entry_ref.shape[1]
    entries = slabs * slab
    pixels = target_ref.shape[2]
    chunks = pixels // LANES
    groups = entries // 8
    tile = where_ref[0]
    length = length_ref[tile]
    view = view_ref[tile]
    values = [
        jnp.concatenate([entry_ref[j * 10 + p : j * 10 + p + 1, :] for j in range(slabs)], axis=1)
        for p in range(10)
    ]

    first = [cam_ref[view, 0, j] for j in range(4)]
    second = [cam_ref[view, 1, j] for j in range(4)]
    variance = [jnp.exp(2.0 * values[3 + j]) for j in range(3)]
    half = 0.5 * TILE_SIDE
    center_x = first[0] * values[0] + first[1] * values[1] + first[2] * values[2] + first[3] + half
    center_y = second[0] * values[0] + second[1] * values[1] + second[2] * values[2] + second[3] + half
    cov_xx = sum(first[j] * first[j] * variance[j] for j in range(3)) + 0.3
    cov_xy = sum(first[j] * second[j] * variance[j] for j in range(3))
    cov_yy = sum(second[j] * second[j] * variance[j] for j in range(3)) + 0.3
    determinant = cov_xx * cov_yy - cov_xy * cov_xy
    conic_a = cov_yy / determinant
    conic_b = -cov_xy / determinant
    conic_c = cov_xx / determinant
    opacity = 1.0 / (1.0 + jnp.exp(-values[6]))
    place = lax.broadcasted_iota(jnp.int32, (1, entries), 1)
    shown = jnp.where(place < length, opacity, 0.0)
    rows = [center_x, center_y, -0.5 * conic_a, -conic_b, -0.5 * conic_c, shown] + values[7:10]
    table = jnp.concatenate(rows + [jnp.zeros((LANES - len(rows), entries), F32)], axis=0)
    columns[...] = table.T

    lane = lax.broadcasted_iota(jnp.int32, (8, LANES), 1)
    sub = lax.broadcasted_iota(jnp.int32, (8, LANES), 0)
    pixel_x = (lane & (TILE_SIDE - 1)).astype(F32) + 0.5
    pixel_y = (lane >> 5).astype(F32) + 0.5
    rows_chunk = LANES // TILE_SIDE
    ones = jnp.ones((8, LANES), F32)

    def spread(cols, j):
        return jnp.broadcast_to(cols[:, j : j + 1], (8, LANES))

    def forward(g, carry):
        trans, color = carry
        at = pl.ds(pl.multiple_of(g * 8, 8), 8)
        cols = columns[pl.ds(g, 8, stride=groups), :]
        cx, cy, qa, qb, qc, op, red, green, blue = [spread(cols, j) for j in range(9)]
        ex = pixel_x - cx
        ey0 = pixel_y - cy
        qaxx = qa * ex * ex
        qbx = qb * ex
        new_trans, new_color = [], []
        for c in range(chunks):
            ey = ey0 + float(c * rows_chunk)
            alpha = op * jnp.exp(qaxx + (qbx + qc * ey) * ey)
            t = trans[c]
            part = slice(c * LANES, (c + 1) * LANES)
            alphas[at, part] = alpha
            weight = alpha * t
            weights[at, part] = weight
            new_trans.append(t - weight)
            new_color.append(color[3 * c] + weight * red)
            new_color.append(color[3 * c + 1] + weight * green)
            new_color.append(color[3 * c + 2] + weight * blue)
        return new_trans, new_color

    zeros = jnp.zeros((8, LANES), F32)
    trans, color = lax.fori_loop(
        0, groups, forward, ([ones] * chunks, [zeros] * (3 * chunks)), unroll=4
    )

    chosen = lax.broadcasted_iota(jnp.int32, (slabs, LANES), 0) == tile
    behinds = []
    for c in range(chunks):
        part = slice(c * LANES, (c + 1) * LANES)
        run = jnp.where(sub >= 1, pltpu.roll(trans[c], 1, 0), 1.0)
        for s in (1, 2, 4):
            run = run * jnp.where(sub >= s, pltpu.roll(run, s, 0), 1.0)
        carries[:, part] = run
        left = (run * trans[c])[7:8, :]
        total = 0.0
        pulled = zeros
        for k in range(3):
            lit = run * color[3 * c + k]
            shade = jnp.sum(lit, axis=0, keepdims=True) + left * back_ref[k]
            image_ref[k : k + 1, part] = shade
            miss = shade - jnp.sum(
                jnp.where(chosen, target_ref[k, :, part], 0.0), axis=0, keepdims=True
            )
            misses[k, :, part] = jnp.broadcast_to(miss, (8, LANES))
            total = total + miss * shade
            pulled = pulled + miss * lit
        ahead = jnp.where(sub >= 1, pltpu.roll(pulled, 1, 0), 0.0)
        for s in (1, 2, 4):
            ahead = ahead + jnp.where(sub >= s, pltpu.roll(ahead, s, 0), 0.0)
        behinds.append(total - ahead)

    def backward(g, behind):
        at = pl.ds(pl.multiple_of(g * 8, 8), 8)
        spaced = pl.ds(g, 8, stride=groups)
        cols = columns[spaced, :]
        cx, cy, red, green, blue = [spread(cols, j) for j in (0, 1, 6, 7, 8)]
        ex = pixel_x - cx
        ey0 = pixel_y - cy
        new_behind = []
        acc = [zeros] * 6
        for c in range(chunks):
            part = slice(c * LANES, (c + 1) * LANES)
            alpha = alphas[at, part]
            weight = weights[at, part] * carries[:, part]
            m0, m1, m2 = misses[0, :, part], misses[1, :, part], misses[2, :, part]
            pull = m0 * red + m1 * green + m2 * blue
            rest = behind[c] - weight * pull
            new_behind.append(rest)
            grad = weight * pull - rest * (alpha / (1.0 - alpha))
            ey = ey0 + float(c * rows_chunk)
            gy = grad * ey
            acc[0] = acc[0] + grad
            acc[1] = acc[1] + gy
            acc[2] = acc[2] + gy * ey
            acc[3] = acc[3] + weight * m0
            acc[4] = acc[4] + weight * m1
            acc[5] = acc[5] + weight * m2
        gx = acc[0] * ex
        fields = [acc[0], gx, acc[1], gx * ex, acc[1] * ex, acc[2], acc[3], acc[4], acc[5]]
        packed = zeros
        for j, field in enumerate(fields):
            packed = jnp.where(lane == j, jnp.sum(field, axis=1, keepdims=True), packed)
        sums[spaced, :] = packed
        return new_behind

    lax.fori_loop(0, groups, backward, behinds, unroll=4)

    flat = sums[...].T
    s0, sx, sy, sxx, sxy, syy, d_red, d_green, d_blue = [flat[j : j + 1, :] for j in range(9)]
    d_x = conic_a * sx + conic_b * sy
    d_y = conic_b * sx + conic_c * sy
    d_a, d_b, d_c = -0.5 * sxx, -sxy, -0.5 * syy
    d_xx = -(conic_a * conic_a * d_a + conic_a * conic_b * d_b + conic_b * conic_b * d_c)
    d_yy = -(conic_b * conic_b * d_a + conic_b * conic_c * d_b + conic_c * conic_c * d_c)
    d_xy = -(
        2.0 * conic_a * conic_b * d_a
        + (conic_a * conic_c + conic_b * conic_b) * d_b
        + 2.0 * conic_b * conic_c * d_c
    )
    out = [first[j] * d_x + second[j] * d_y for j in range(3)]
    for j in range(3):
        d_var = first[j] * first[j] * d_xx + first[j] * second[j] * d_xy + second[j] * second[j] * d_yy
        out.append(2.0 * variance[j] * d_var)
    out += [s0 * (1.0 - opacity), d_red, d_green, d_blue]
    out = jnp.concatenate(out, axis=0)
    for j in range(slabs):
        grad_ref[j * 10 : (j + 1) * 10, :] = out[:, j * slab : (j + 1) * slab]


def collect_kernel(
    tiles, depths, own_ref, image_ref, lists_ref, gradient_ref, picture_ref,
    images_ref, out_ref, inbox, partial, pieces, mine,
    send, receive, image_send, image_recv, image_own, cut_send, cut_recv, all_send, all_recv,
):
    lines = out_ref.shape[0]
    highs = lines // 10
    quarter = lines // depths
    slabs, slab = lists_ref.shape[1], lists_ref.shape[3]
    entries = slabs * slab
    me_t, me_d = lax.axis_index("tile"), lax.axis_index("depth")

    def along(step):
        return {"depth": lax.rem(me_d + step, depths)}

    def across(step):
        return {"tile": lax.rem(me_t + step, tiles)}

    def grads(step):
        return remote(own_ref, inbox.at[step], send.at[step], receive.at[step], across(step))

    greet([across(s) for s in range(1, tiles)] + [along(s) for s in range(1, depths)])
    for step in range(tiles - 1, 0, -1):
        grads(step).start()
    image_copies = [
        remote(image_ref, images_ref.at[me_d], image_send.at[s], image_recv.at[s], along(s))
        for s in range(1, depths)
    ]
    image_copies.append(pltpu.make_async_copy(image_ref, images_ref.at[me_d], image_own))
    for copy in image_copies:
        copy.start()

    high_iota = lax.broadcasted_iota(jnp.int32, (highs, entries), 0)
    low_iota = lax.broadcasted_iota(jnp.int32, (LANES, entries), 0)

    def placed(block, slot):
        owner, row = entry_rows(lists_ref, slot)
        onehot = jnp.where(low_iota == (row & (LANES - 1)), 1.0, 0.0).astype(BF16)
        mask = high_iota == jnp.where(owner == me_t, row >> 7, -1)
        wide = jnp.concatenate([block[j * 10 : (j + 1) * 10, :] for j in range(slabs)], axis=1)
        spots = jnp.concatenate(
            [jnp.where(mask, wide[p : p + 1, :], 0.0) for p in range(10)], axis=0
        )
        high = spots.astype(BF16)
        middle = (spots - high.astype(F32)).astype(BF16)
        dims = (((1,), (1,)), ((), ()))
        return lax.dot_general(
            high, onehot, dims, preferred_element_type=F32
        ) + lax.dot_general(middle, onehot, dims, preferred_element_type=F32)

    partial[...] = placed(own_ref[...], me_t)

    def add(step, carry):
        grads(step).wait()
        partial[...] += placed(inbox[step], lax.rem(me_t - step + tiles, tiles))
        return carry

    lax.fori_loop(1, tiles, add, 0, unroll=tiles - 1 if tiles <= 8 else 1)
    for copy in image_copies:
        copy.wait()

    def rows_of(index):
        return pl.ds(pl.multiple_of(index * quarter, 8), quarter)

    cuts = [
        remote(
            partial.at[rows_of(lax.rem(me_d + s, depths))], pieces.at[s],
            cut_send.at[s], cut_recv.at[s], along(s),
        )
        for s in range(1, depths)
    ]
    for copy in cuts:
        copy.start()
    total = partial[rows_of(me_d), :]
    for s, copy in enumerate(cuts):
        copy.wait()
        total = total + pieces[s + 1]
    mine[...] = total
    shares = [
        remote(mine, out_ref.at[rows_of(me_d)], all_send.at[s], all_recv.at[s], along(s))
        for s in range(1, depths)
    ]
    for copy in shares:
        copy.start()
    out_ref[rows_of(me_d), :] = total
    for d in range(depths):
        for k in range(3):
            picture_ref[k, d : d + 1, :] = images_ref[d, k : k + 1, :]
    for copy in shares:
        copy.wait()
    for p in range(10):
        for h in range(highs):
            line = p * highs + h
            gradient_ref[p : p + 1, h * LANES : (h + 1) * LANES] = out_ref[line : line + 1, :]


def adam_update(param, first, second, gradient):
    new_first = 0.9 * first + 0.1 * gradient
    new_second = 0.999 * second + 0.001 * gradient * gradient
    corrected = new_first / (1.0 - 0.9**10) / (jnp.sqrt(new_second / (1.0 - 0.999**10)) + 1e-08)
    return (param - 0.05 * corrected, new_first, new_second)


def body(
    positions, log_scales, opacity_logits, colors, first_moment, second_moment,
    cameras, background, target, tile_view, tile_length, list_owner, list_row,
):
    tiles_here, _, pixels = target.shape
    slab = list_row.shape[2]
    depth_count = lax.axis_size("depth")
    entries = slab * depth_count
    here = lax.axis_index("depth").astype(jnp.int32).reshape(1)
    assert tiles_here == depth_count
    params = jnp.concatenate([positions, log_scales, opacity_logits, colors], axis=0)
    splats = params.shape[1]
    lines = 10 * splats // LANES
    tile_count = lax.axis_size("tile")
    assert 10 * slab * depth_count % LANES == 0 and slab == LANES
    smem = pl.BlockSpec(memory_space=pltpu.SMEM)
    vmem = pl.BlockSpec(memory_space=pltpu.VMEM)
    dma = pltpu.SemaphoreType.DMA
    block = (10 * depth_count, slab)
    limit = 60 << 20
    lists, entry = pl.pallas_call(
        functools.partial(fetch_kernel, tile_count, depth_count),
        out_shape=[
            jax.ShapeDtypeStruct((tile_count, depth_count, 2, slab), jnp.int32),
            jax.ShapeDtypeStruct(block, F32),
        ],
        in_specs=[vmem] * 6,
        out_specs=[vmem] * 2,
        scratch_shapes=[
            pltpu.VMEM((depth_count, 2, slab), jnp.int32),
            pltpu.VMEM((lines, LANES), F32),
            pltpu.VMEM((lines, 2 * LANES), BF16),
            pltpu.VMEM((lines, LANES), BF16),
            pltpu.VMEM((tile_count,) + block, F32),
            pltpu.VMEM((tile_count,) + block, F32),
            dma((tile_count, depth_count)),
            dma((tile_count, depth_count)),
            dma,
            dma((tile_count,)),
            dma((tile_count,)),
        ],
        name="fetch",
        compiler_params=pltpu.CompilerParams(
            collective_id=1, has_side_effects=True, vmem_limit_bytes=limit
        ),
    )(
        list_owner.reshape(tiles_here, 1, slab), list_row[0],
        positions, log_scales, opacity_logits, colors,
    )
    own_image, own_grad = pl.pallas_call(
        render_kernel,
        out_shape=[
            jax.ShapeDtypeStruct((3, pixels), F32),
            jax.ShapeDtypeStruct(block, F32),
        ],
        in_specs=[smem] * 5 + [vmem] * 2,
        out_specs=[vmem] * 2,
        scratch_shapes=[
            pltpu.VMEM((entries, pixels), F32),
            pltpu.VMEM((entries, pixels), F32),
            pltpu.VMEM((3, 8, pixels), F32),
            pltpu.VMEM((8, pixels), F32),
            pltpu.VMEM((entries, LANES), F32),
            pltpu.VMEM((entries, LANES), F32),
        ],
        name="render",
        compiler_params=pltpu.CompilerParams(vmem_limit_bytes=limit),
    )(here, tile_view, tile_length, cameras, background, entry, target.transpose(1, 0, 2))
    quarter = lines // depth_count
    gradient, picture = pl.pallas_call(
        functools.partial(collect_kernel, tile_count, depth_count),
        out_shape=[
            jax.ShapeDtypeStruct((10, splats), F32),
            jax.ShapeDtypeStruct((3, depth_count, pixels), F32),
        ],
        in_specs=[vmem] * 3,
        out_specs=[vmem] * 2,
        scratch_shapes=[
            pltpu.VMEM((depth_count, 3, pixels), F32),
            pltpu.VMEM((lines, LANES), F32),
            pltpu.VMEM((tile_count,) + block, F32),
            pltpu.VMEM((lines, LANES), F32),
            pltpu.VMEM((depth_count, quarter, LANES), F32),
            pltpu.VMEM((quarter, LANES), F32),
            dma((tile_count,)),
            dma((tile_count,)),
            dma((depth_count,)),
            dma((depth_count,)),
            dma,
            dma((depth_count,)),
            dma((depth_count,)),
            dma((depth_count,)),
            dma((depth_count,)),
        ],
        name="collect",
        compiler_params=pltpu.CompilerParams(
            collective_id=2, has_side_effects=True, vmem_limit_bytes=limit
        ),
    )(own_grad, own_image, lists)
    image = picture.transpose(1, 0, 2)
    new_params, new_first, new_second = adam_update(params, first_moment, second_moment, gradient)
    return (image, new_params, new_first, new_second)


def solution(mesh):
    placed = (
        P(None, "tile"),
        P(None, "tile"),
        P(None, "tile"),
        P(None, "tile"),
        P(None, "tile"),
        P(None, "tile"),
        P(),
        P(),
        P("tile", None, None),
        P("tile"),
        P("tile"),
        P("depth", "tile", None, None),
        P("depth", "tile", None),
    )
    return jax.shard_map(
        body,
        mesh=mesh,
        in_specs=placed,
        out_specs=(P("tile", None, None), P(None, "tile"), P(None, "tile"), P(None, "tile")),
        check_vma=False,
    )
```
